32 devices in a mesh: ctx: 8 (over z, x), wa: 4 (over y, core).
Axes of the slice: x: 2, y: 2, z: 4, core: 2. Of those that a mesh axis runs over, the one named last changes fastest.
Arguments:
- inputs: bfloat16 [4, 1024, 2048], P('wa', 'ctx'), may hold values from -6 to 6
- ln_gain: bfloat16 [2048], P('wa'), may hold values from 0.5 to 1.5
- ln_bias: bfloat16 [2048], P('wa'), may hold values from -1.75 to 1.75
- w_qkv: bfloat16 [2048, 6144], P('wa'), may hold values from -0.1875 to 0.1875
- b_qkv: bfloat16 [6144], P('wa'), may hold values from -1.75 to 1.75
- w_out: bfloat16 [2048, 2048], P('wa'), may hold values from -0.5 to 0.5
- b_out: bfloat16 [2048], P('wa'), may hold values from -1.75 to 1.75
- w_fc1: bfloat16 [8192, 2048], P('wa'), may hold values from -0.125 to 0.125
- b_fc1: bfloat16 [8192], P('wa'), may hold values from -1.75 to 1.75
- w_fc2: bfloat16 [8192, 2048], P('wa'), may hold values from -0.0625 to 0.0625
- b_fc2: bfloat16 [2048], P('wa'), may hold values from -1.75 to 1.75
- cotangent: bfloat16 [4, 1024, 2048], P('wa', 'ctx'), may hold values from -8 to 8
Outputs:
- outputs: bfloat16 [4, 1024, 2048], P('wa', 'ctx')
- input_grads: bfloat16 [4, 1024, 2048], P('wa', 'ctx')
- grad_ln_gain: float32 [2048], P(('ctx', 'wa'))
- grad_ln_bias: float32 [2048], P(('ctx', 'wa'))
- grad_qkv: float32 [2048, 6144], P(('ctx', 'wa'))
- grad_b_qkv: float32 [6144], P(('ctx', 'wa'))
- grad_out: float32 [2048, 2048], P(('ctx', 'wa'))
- grad_b_out: float32 [2048], P(('ctx', 'wa'))
- grad_fc1: float32 [8192, 2048], P('wa', 'ctx')
- grad_b_fc1: float32 [8192], P('wa')
- grad_fc2: float32 [8192, 2048], P('wa', 'ctx')
- grad_b_fc2: float32 [2048], P(('ctx', 'wa'))
The draws below stay inside these ranges and needn't reach their ends.
All inputs are finite; a program needn't handle non-finite values.
Results may differ from the reference program's by a relative error of at most 0.017.
Values may be sent and summed in bfloat16 or wider, within the bound.
No kernel may reach another device: no remote copies, remote signals or barrier semaphores. Data moves between devices by JAX's collectives and lax.ppermute only.
A program may use at most 704 MiB of HBM per device.

```python
import jax
import jax.numpy as jnp
from jax import lax

D = 2048
HEADS = 32
HEAD_DIM = 64
ROT = 32
FF = 8192
SEQ = 1024
SEQS = 4


def strengthened(values, own_key, source, target, parts, factor):
    owner, partner = [(jnp.arange(values.shape[axis_at]) // (values.shape[axis_at] // parts)).reshape([-1 if axis == axis_at else 1 for axis in range(values.ndim)]) for axis_at in (source, target)]
    chosen = jax.random.permutation(own_key, parts)[partner]
    strong = (owner == chosen) | (owner == (partner + parts // 2) % parts)
    return jnp.where(strong, factor * values, values)


def level_of(stream_key, dims, shards, low, top_value):
    loudness = 1.0
    for axis_at, blocks in shards:
        heights = jax.random.uniform(jax.random.fold_in(jax.random.fold_in(stream_key, 6), axis_at), (blocks,), jnp.float32, low / len(shards), top_value / len(shards))
        loudness = loudness * jnp.repeat(jnp.exp(heights), dims[axis_at] // blocks).reshape((-1,) + (1,) * (len(dims) - 1 - axis_at))
    return loudness


def scatter_about(own_key, dims, scale, reach, pieces=(), held_as=jnp.bfloat16):
    array = scale * jax.random.normal(own_key, dims, jnp.float32)
    if pieces:
        array = array * level_of(own_key, dims, pieces, -0.22, 0.18)
    return jnp.clip(array, -reach, reach).astype(held_as)


def heavy_noise(own_key, extent, deviation, limit, cuts, heavy, kind=jnp.bfloat16):
    drawn = deviation * jax.random.normal(own_key, extent, jnp.float32)
    if cuts:
        drawn = drawn * level_of(own_key, extent, cuts, -0.22, 0.18)
    return jnp.clip(strengthened(drawn, jax.random.fold_in(own_key, 3), *heavy), -limit, limit).astype(kind)


def setup_inputs(seed: int = 0) -> dict:
    splits = jax.random.split(jax.random.key(seed), 13)
    return {
        "inputs": scatter_about(splits[0], (SEQS, SEQ, D), 1.0, 6.0, ((0, 4), (1, 8))),
        "ln_gain": jnp.clip(1.0 + 0.1 * jax.random.normal(splits[1], (D,), jnp.float32), 0.5, 1.5).astype(jnp.bfloat16),
        "ln_bias": scatter_about(splits[2], (D,), 0.3, 1.75, ((0, 4),)),
        "w_qkv": scatter_about(splits[3], (D, 3 * D), (D // 2) ** -0.5, 0.1875, ((0, 4),)),
        "b_qkv": scatter_about(splits[4], (3 * D,), 0.3, 1.75, ((0, 4),)),
        "w_out": scatter_about(splits[5], (D, D), (D // 16) ** -0.5, 0.5, ((0, 4),)),
        "b_out": scatter_about(splits[6], (D,), 0.3, 1.75, ((0, 4),)),
        "w_fc1": scatter_about(splits[7], (FF, D), D ** -0.5, 0.125, ((0, 4),)),
        "b_fc1": scatter_about(splits[8], (FF,), 0.3, 1.75, ((0, 4),)),
        "w_fc2": scatter_about(splits[9], (FF, D), FF ** -0.5, 0.0625, ((0, 4),)),
        "b_fc2": scatter_about(splits[10], (D,), 0.3, 1.75, ((0, 4),)),
        "cotangent": heavy_noise(splits[11], (SEQS, SEQ, D), 1.0, 8.0, ((0, 4), (1, 8)), (1, 2, 8, 2.0)),
    }


@jax.custom_vjp
def low(v):
    return lax.optimization_barrier(v.astype(jnp.bfloat16)).astype(jnp.float32)

@jax.custom_vjp
def low_back(v):
    return v

def low_keep(v):
    return (low(v), None)

def low_pass(kept, grad):
    return (grad,)

def back_keep(v):
    return (v, None)

def back_low(kept, grad):
    return (low(grad),)
low.defvjp(low_keep, low_pass)
low_back.defvjp(back_keep, back_low)
highest = lax.Precision.HIGHEST
eps_norm = 1e-05
rope_base = 10000.0
key_block = 512
neg_large = -1e+30
gelu_coeff = 0.7978845608028654

def gelu_tanh(pre_act):
    return 0.5 * pre_act * (1.0 + jnp.tanh(gelu_coeff * (pre_act + 0.044715 * pre_act * pre_act * pre_act)))

def rope_tables(positions):
    half_rot = ROT // 2
    inverse_freq = rope_base ** (-(jnp.arange(half_rot).astype(jnp.float32) * (2.0 / ROT)))
    angles = positions[:, None] * inverse_freq[None, :]
    angles = jnp.concatenate([angles, angles], axis=1)
    return (jnp.cos(angles), jnp.sin(angles))

def rotate(head_rows, cosine, sine_table):
    half_rot = ROT // 2
    rotary = head_rows[..., :ROT]
    turned = jnp.concatenate([-rotary[..., half_rot:], rotary[..., :half_rot]], axis=-1)
    rotary = rotary * cosine[:, None, :] + turned * sine_table[:, None, :]
    return jnp.concatenate([rotary, head_rows[..., ROT:]], axis=-1)

def attention(queries, key_rows, value_rows):
    query_rows = min(key_block, SEQ)
    score_scale = HEAD_DIM ** (-0.5)
    key_pos = jnp.arange(SEQ, dtype=jnp.int32)

    def one_block(block_index):
        first_row = block_index * query_rows
        block_queries = lax.dynamic_slice_in_dim(queries, first_row, query_rows, 0)
        raw_scores = low_back(jnp.einsum('qhd,khd->hqk', block_queries, key_rows, precision=highest))
        query_pos = first_row + jnp.arange(query_rows, dtype=jnp.int32)
        allowed = key_pos[None, :] <= query_pos[:, None]
        scores = jnp.where(allowed[None], raw_scores * score_scale, neg_large)
        row_peak = lax.optimization_barrier(jnp.max(scores, axis=-1, keepdims=True))
        exp_scores = jnp.exp(scores - row_peak)
        probabilities = low(exp_scores / lax.optimization_barrier(jnp.sum(exp_scores, axis=-1, keepdims=True)))
        return jnp.einsum('hqk,khd->qhd', probabilities, value_rows, precision=highest)
    blocks = lax.map(jax.checkpoint(one_block), jnp.arange(SEQ // query_rows, dtype=jnp.int32))
    return blocks.reshape(SEQ, HEADS * HEAD_DIM)

def forward(tokens, ln_gain, ln_bias, w_qkv, b_qkv, w_out, b_out, w_fc1, b_fc1, w_fc2, b_fc2):
    model_width = HEADS * HEAD_DIM
    centre = lax.optimization_barrier(jnp.mean(tokens, axis=1, keepdims=True))
    centred = tokens - centre
    inverse = lax.rsqrt(lax.optimization_barrier(jnp.mean(centred * centred, axis=1, keepdims=True)) + eps_norm)
    normed = low(centred * inverse * ln_gain + ln_bias)
    projected = low_back(jnp.dot(normed, w_qkv, precision=highest) + b_qkv)
    cosine, sine_table = rope_tables(jnp.arange(SEQ).astype(jnp.float32))
    head_shape = (SEQ, HEADS, HEAD_DIM)
    queries = low(rotate(projected[:, :model_width].reshape(head_shape), cosine, sine_table))
    key_rows = low(rotate(projected[:, model_width:2 * model_width].reshape(head_shape), cosine, sine_table))
    value_rows = low(projected[:, 2 * model_width:].reshape(head_shape))
    attended = low_back(low(attention(queries, key_rows, value_rows)))
    branch_attn = jnp.dot(attended, w_out, precision=highest) + b_out
    hidden = low_back(jnp.dot(normed, w_fc1.T, precision=highest) + b_fc1)
    gated_act = low_back(low(gelu_tanh(hidden)))
    branch_mlp = jnp.dot(gated_act, w_fc2, precision=highest) + b_fc2
    return tokens + branch_attn + branch_mlp

def reference(inputs, ln_gain, ln_bias, w_qkv, b_qkv, w_out, b_out, w_fc1, b_fc1, w_fc2, b_fc2, cotangent):
    params = tuple((item.astype(jnp.float32) for item in (ln_gain, ln_bias, w_qkv, b_qkv, w_out, b_out, w_fc1, b_fc1, w_fc2, b_fc2)))

    def per_sequence(totals, paired):
        seq_inputs, seq_cotangent = paired
        results, pullback = jax.vjp(forward, seq_inputs.astype(jnp.float32), *params)
        grads = pullback(seq_cotangent.astype(jnp.float32))
        new_totals = tuple((older + newer for older, newer in zip(totals, grads[1:])))
        return (new_totals, (results.astype(jnp.bfloat16), grads[0].astype(jnp.bfloat16)))
    zeros_init = tuple((jnp.zeros(item.shape, jnp.float32) for item in params))
    totals, (outputs, input_grads) = lax.scan(per_sequence, zeros_init, (inputs, cotangent))
    return (outputs, input_grads, totals[0], totals[1], totals[2], totals[3], totals[4], totals[5], totals[6], totals[7], totals[8], totals[9])
```

```python
import math

import jax
import jax.numpy as jnp
from jax import lax
from jax.experimental import pallas as pl
from jax.experimental.pallas import tpu as pltpu
from jax.sharding import PartitionSpec as P

HEADS = 32
HEAD_DIM = 64
ROT = 32


eps_norm = 1e-05
rope_base = 10000.0
key_block = 512
neg_large = -1e30
gelu_coeff = 0.7978845608028654


def gelu_tanh(pre_act):
    return (
        0.5
        * pre_act
        * (1.0 + jnp.tanh(gelu_coeff * (pre_act + 0.044715 * pre_act * pre_act * pre_act)))
    )


def rope_tables(positions):
    half_rot = ROT // 2
    inverse_freq = rope_base ** (-(jnp.arange(half_rot).astype(jnp.float32) * (2.0 / ROT)))
    angles = positions[:, None] * inverse_freq[None, :]
    angles = jnp.concatenate([angles, angles], axis=1)
    return (jnp.cos(angles), jnp.sin(angles))


def rotate(head_rows, cosine, sine_table):
    half_rot = ROT // 2
    rotary = head_rows[..., :ROT]
    turned = jnp.concatenate([-rotary[..., half_rot:], rotary[..., :half_rot]], axis=-1)
    rotary = rotary * cosine[:, None, :] + turned * sine_table[:, None, :]
    return jnp.concatenate([rotary, head_rows[..., ROT:]], axis=-1)


def unrotate(grad_rows, cosine, sine_table):
    half_rot = ROT // 2
    rotary = grad_rows[..., :ROT]
    moved = rotary * sine_table[:, None, :]
    turned = jnp.concatenate([moved[..., half_rot:], -moved[..., :half_rot]], axis=-1)
    rotary = rotary * cosine[:, None, :] + turned
    return jnp.concatenate([rotary, grad_rows[..., ROT:]], axis=-1)


def unchanged(current):
    return current


def on_device(
    inputs, ln_gain, ln_bias, w_qkv, b_qkv, w_out, b_out, w_fc1, b_fc1, w_fc2, b_fc2, cotangent
):
    tokens = inputs[0].astype(jnp.float32)
    token_count, model_width = tokens.shape
    contract_rows = (((0,), (0,)), ((), ()))
    contract_cols = (((1,), (1,)), ((), ()))
    gain_all, shift_all, qkv_weight, qkv_bias, out_weight, out_bias, second_bias = (
        lax.all_gather(ln_gain, "wa", axis=0, tiled=True),
        lax.all_gather(ln_bias, "wa", axis=0, tiled=True),
        lax.all_gather(w_qkv, "wa", axis=0, tiled=True),
        lax.all_gather(b_qkv, "wa", axis=0, tiled=True),
        lax.all_gather(w_out, "wa", axis=0, tiled=True),
        lax.all_gather(b_out, "wa", axis=0, tiled=True),
        lax.all_gather(b_fc2, "wa", axis=0, tiled=True),
    )
    centre = jnp.mean(tokens, axis=1, keepdims=True)
    centred = tokens - centre
    inverse = lax.rsqrt(jnp.mean(centred * centred, axis=1, keepdims=True) + eps_norm)
    scaled = centred * inverse
    normed = (scaled * gain_all + shift_all).astype(jnp.bfloat16)
    projected = jnp.dot(normed, qkv_weight, preferred_element_type=jnp.float32) + qkv_bias
    offset = lax.axis_index("ctx") * token_count
    query_pos = offset + jnp.arange(token_count, dtype=jnp.int32)
    last_query = offset + token_count - 1
    cosine, sine_table = rope_tables(query_pos.astype(jnp.float32))
    head_shape = (token_count, HEADS, HEAD_DIM)
    queries = rotate(projected[:, :model_width].reshape(head_shape), cosine, sine_table).astype(
        jnp.bfloat16
    )
    key_rows = (
        rotate(projected[:, model_width : 2 * model_width].reshape(head_shape), cosine, sine_table)
        .astype(jnp.bfloat16)
        .reshape(token_count, model_width)
    )
    value_rows = projected[:, 2 * model_width :].astype(jnp.bfloat16)
    score_scale = HEAD_DIM ** (-0.5)
    start_state = (
        jnp.full((HEADS, token_count), neg_large, jnp.float32),
        jnp.zeros((HEADS, token_count), jnp.float32),
        jnp.zeros((token_count, HEADS, HEAD_DIM), jnp.float32),
    )
    running = start_state
    key_part = lax.all_gather(key_rows, "ctx", axis=0, tiled=True)
    value_part = lax.all_gather(value_rows, "ctx", axis=0, tiled=True)
    row_count = key_part.shape[0]
    block_rows = math.gcd(row_count, key_block)
    block_count = row_count // block_rows
    key_blocks = key_part.reshape(block_count, block_rows, HEADS, HEAD_DIM)
    value_blocks = value_part.reshape(block_count, block_rows, HEADS, HEAD_DIM)

    def visit_block(current, block_items):
        block_index, key_slab, value_slab = block_items
        start_row = block_index * block_rows

        def attend(state_now):
            row_peak, row_total, weighted = state_now
            raw_scores = jnp.einsum(
                "qhd,khd->hqk", queries, key_slab, preferred_element_type=jnp.float32
            )
            key_pos = start_row + jnp.arange(block_rows, dtype=jnp.int32)
            allowed = (key_pos[None, :] <= query_pos[:, None])[None]
            scores = jnp.where(allowed, raw_scores * score_scale, neg_large)
            new_peak = jnp.maximum(row_peak, jnp.max(scores, axis=2))
            factor = jnp.exp(row_peak - new_peak)
            exp_scores = jnp.where(allowed, jnp.exp(scores - new_peak[:, :, None]), 0.0)
            row_total = row_total * factor + jnp.sum(exp_scores, axis=2)
            weighted = weighted * jnp.transpose(factor)[:, :, None] + jnp.einsum(
                "hqk,khd->qhd",
                exp_scores.astype(jnp.bfloat16),
                value_slab,
                preferred_element_type=jnp.float32,
            )
            return (new_peak, row_total, weighted)

        return (lax.cond(start_row <= last_query, attend, unchanged, current), None)

    running, ignored = lax.scan(
        visit_block, running, (jnp.arange(block_count, dtype=jnp.int32), key_blocks, value_blocks)
    )
    row_peak, row_total, weighted = running
    log_total = row_peak + jnp.log(row_total)
    attended_f32 = weighted / jnp.transpose(row_total)[:, :, None]
    attended = attended_f32.reshape(token_count, model_width).astype(jnp.bfloat16)
    branch_attn = jnp.dot(attended, out_weight, preferred_element_type=jnp.float32) + out_bias
    upstream = cotangent[0]
    upstream_f32 = upstream.astype(jnp.float32)
    fc1_all, fc1_bias_all, fc2_all = (
        lax.all_gather(w_fc1, "wa", axis=0, tiled=True),
        lax.all_gather(b_fc1, "wa", axis=0, tiled=True),
        lax.all_gather(w_fc2, "wa", axis=0, tiled=True),
    )
    hidden = (
        lax.dot_general(normed, fc1_all, contract_cols, preferred_element_type=jnp.float32)
        + fc1_bias_all
    )
    gated_act = gelu_tanh(hidden).astype(jnp.bfloat16)
    branch_mlp = jnp.dot(gated_act, fc2_all, preferred_element_type=jnp.float32) + second_bias
    outputs = (tokens + branch_attn + branch_mlp).astype(jnp.bfloat16)[None]
    grad_gated = lax.dot_general(
        upstream, fc2_all, contract_cols, preferred_element_type=jnp.float32
    ).astype(jnp.bfloat16)
    fc2_term = lax.dot_general(
        gated_act, upstream, contract_rows, preferred_element_type=jnp.float32
    )
    ignored, slope_fn = jax.vjp(gelu_tanh, hidden)
    grad_hidden = slope_fn(grad_gated.astype(jnp.float32))[0].astype(jnp.bfloat16)
    fc1_bias_term = jnp.sum(grad_hidden.astype(jnp.float32), axis=0)
    fc1_term = lax.dot_general(
        grad_hidden, normed, contract_rows, preferred_element_type=jnp.float32
    )
    grad_normed_mlp = jnp.dot(grad_hidden, fc1_all, preferred_element_type=jnp.float32)
    fc1_share, fc2_share, bias_share = (
        lax.psum_scatter(
            fc1_term.astype(jnp.bfloat16), "wa", scatter_dimension=0, tiled=True
        ).astype(jnp.float32),
        lax.psum_scatter(
            fc2_term.astype(jnp.bfloat16), "wa", scatter_dimension=0, tiled=True
        ).astype(jnp.float32),
        lax.psum_scatter(
            fc1_bias_term.astype(jnp.bfloat16), "wa", scatter_dimension=0, tiled=True
        ).astype(jnp.float32),
    )
    grad_fc1, grad_fc2 = (
        lax.psum_scatter(
            fc1_share.astype(jnp.bfloat16), "ctx", scatter_dimension=1, tiled=True
        ).astype(jnp.float32),
        lax.psum_scatter(
            fc2_share.astype(jnp.bfloat16), "ctx", scatter_dimension=1, tiled=True
        ).astype(jnp.float32),
    )
    grad_b_fc1 = lax.psum(bias_share, "ctx")
    out_term = lax.dot_general(
        attended, upstream, contract_rows, preferred_element_type=jnp.float32
    )
    bias_term = jnp.sum(upstream_f32, axis=0)
    grad_attended = (
        lax.dot_general(upstream, out_weight, contract_cols, preferred_element_type=jnp.float32)
        .astype(jnp.bfloat16)
        .reshape(head_shape)
    )
    row_deltas = jnp.transpose(jnp.sum(grad_attended.astype(jnp.float32) * attended_f32, axis=2))
    keys_all, values_all = (
        lax.all_gather(key_rows, "ctx", axis=0, tiled=True),
        lax.all_gather(value_rows, "ctx", axis=0, tiled=True),
    )
    sequence_rows = keys_all.shape[0]

    def block_scores(key_slab, value_slab, start_row, block_rows):
        raw_scores = jnp.einsum(
            "qhd,khd->hqk", queries, key_slab, preferred_element_type=jnp.float32
        )
        key_pos = start_row + jnp.arange(block_rows, dtype=jnp.int32)
        allowed = (key_pos[None, :] <= query_pos[:, None])[None]
        probabilities = jnp.where(
            allowed, jnp.exp(raw_scores * score_scale - log_total[:, :, None]), 0.0
        )
        grad_probs = jnp.einsum(
            "qhd,khd->hqk", grad_attended, value_slab, preferred_element_type=jnp.float32
        )
        grad_raw = (probabilities * (grad_probs - row_deltas[:, :, None]) * score_scale).astype(
            jnp.bfloat16
        )
        return (probabilities, grad_raw)

    def slabs_at(start_row, block_rows):
        key_slab = lax.dynamic_slice_in_dim(keys_all, start_row, block_rows, 0).reshape(
            block_rows, HEADS, HEAD_DIM
        )
        value_slab = lax.dynamic_slice_in_dim(values_all, start_row, block_rows, 0).reshape(
            block_rows, HEADS, HEAD_DIM
        )
        return (key_slab, value_slab)

    query_block_rows = math.gcd(sequence_rows, key_block)

    def query_visit(grad_queries, block_index):
        start_row = block_index * query_block_rows

        def accumulate(current):
            key_slab, value_slab = slabs_at(start_row, query_block_rows)
            ignored_probs, grad_raw = block_scores(
                key_slab, value_slab, start_row, query_block_rows
            )
            return current + jnp.einsum(
                "hqk,khd->qhd", grad_raw, key_slab, preferred_element_type=jnp.float32
            )

        return (lax.cond(start_row <= last_query, accumulate, unchanged, grad_queries), None)

    grad_queries, ignored = lax.scan(
        query_visit,
        jnp.zeros(head_shape, jnp.float32),
        jnp.arange(sequence_rows // query_block_rows, dtype=jnp.int32),
    )
    row_count = lax.axis_size("ctx") * token_count
    key_block_rows = math.gcd(row_count, key_block)

    def term_visit(dummy, block_index):
        start_row = block_index * key_block_rows

        def contribute(operand):
            key_slab, value_slab = slabs_at(start_row, key_block_rows)
            probabilities, grad_raw = block_scores(key_slab, value_slab, start_row, key_block_rows)
            grad_key_slab = jnp.einsum(
                "hqk,qhd->khd", grad_raw, queries, preferred_element_type=jnp.float32
            ).reshape(key_block_rows, model_width)
            grad_value_slab = jnp.einsum(
                "hqk,qhd->khd",
                probabilities.astype(jnp.bfloat16),
                grad_attended,
                preferred_element_type=jnp.float32,
            ).reshape(key_block_rows, model_width)
            return jnp.concatenate([grad_key_slab, grad_value_slab], axis=1)

        def nothing(operand):
            return jnp.zeros((key_block_rows, 2 * model_width), jnp.float32)

        return (dummy, lax.cond(start_row <= last_query, contribute, nothing, 0))

    dummy, stacked = lax.scan(
        term_visit, 0, jnp.arange(row_count // key_block_rows, dtype=jnp.int32)
    )
    key_grads = lax.psum_scatter(
        stacked.reshape(row_count, 2 * model_width).astype(jnp.bfloat16),
        "ctx",
        scatter_dimension=0,
        tiled=True,
    ).astype(jnp.float32)
    grad_keys = unrotate(
        key_grads[:, :model_width].reshape(head_shape), cosine, sine_table
    ).reshape(token_count, model_width)
    grad_values = key_grads[:, model_width:]
    grad_query_pre = unrotate(grad_queries, cosine, sine_table).reshape(token_count, model_width)
    grad_projected = jnp.concatenate([grad_query_pre, grad_keys, grad_values], axis=1).astype(
        jnp.bfloat16
    )
    qkv_term = lax.dot_general(
        normed, grad_projected, contract_rows, preferred_element_type=jnp.float32
    )
    qkv_bias_term = jnp.sum(grad_projected.astype(jnp.float32), axis=0)
    grad_normed = (
        lax.dot_general(
            grad_projected, qkv_weight, contract_cols, preferred_element_type=jnp.float32
        )
        + grad_normed_mlp
    )
    gain_term = jnp.sum(grad_normed * scaled, axis=0)
    shift_term = jnp.sum(grad_normed, axis=0)
    grad_scaled = grad_normed * gain_all
    grad_inputs = inverse * (
        grad_scaled
        - jnp.mean(grad_scaled, axis=1, keepdims=True)
        - scaled * jnp.mean(grad_scaled * scaled, axis=1, keepdims=True)
    )
    input_grads = (upstream_f32 + grad_inputs).astype(jnp.bfloat16)[None]
    grad_ln_gain, grad_ln_bias, grad_qkv, grad_b_qkv, grad_out, grad_b_out = (
        lax.psum_scatter(gain_term, ("ctx", "wa"), scatter_dimension=0, tiled=True),
        lax.psum_scatter(shift_term, ("ctx", "wa"), scatter_dimension=0, tiled=True),
        lax.psum_scatter(qkv_term, ("ctx", "wa"), scatter_dimension=0, tiled=True),
        lax.psum_scatter(qkv_bias_term, ("ctx", "wa"), scatter_dimension=0, tiled=True),
        lax.psum_scatter(out_term, ("ctx", "wa"), scatter_dimension=0, tiled=True),
        lax.psum_scatter(bias_term, ("ctx", "wa"), scatter_dimension=0, tiled=True),
    )
    return (
        outputs,
        input_grads,
        grad_ln_gain,
        grad_ln_bias,
        grad_qkv,
        grad_b_qkv,
        grad_out,
        grad_b_out,
        grad_fc1,
        grad_b_fc1,
        grad_fc2,
        grad_b_out,
    )


def swap(values, axis, bit):
    return lax.ppermute(values, axis, [(at, at ^ bit) for at in range(lax.axis_size(axis))])


X_BIT, ZLO_BIT, ZHI_BIT = 1, 2, 4
CORE_BIT, Y_BIT = 1, 2
PIECE = 64
PIECES = 16
PAIR = 2 * HEAD_DIM


def swap_x(values):
    return swap(values, "ctx", X_BIT)


def swap_y(values):
    return swap(values, "wa", Y_BIT)


def swap_zhi(values):
    return swap(values, "ctx", ZHI_BIT)


def swap_zlo(values):
    return swap(values, "ctx", ZLO_BIT)


def swap_core(values):
    return swap(values, "wa", CORE_BIT)


def gather_rows(block):
    sides = (block, swap_zhi(block))
    pieces = []
    for side in sides:
        first, second = side[:PIECE], side[PIECE:]
        first_x = swap_x(first)
        second_y = swap_y(second)
        first_y = swap_y(first)
        second_x = swap_x(second)
        first_xy = swap_y(first_x)
        second_xy = swap_x(second_y)
        pieces += [first, first_x, first_y, first_xy, second, second_y, second_x, second_xy]
    return jnp.concatenate(pieces, axis=0)


def add_wide(mine, other):
    return mine.astype(jnp.float32) + other.astype(jnp.float32)


def reduce_side(part):
    half = 4 * PIECE
    first, second = part[:half], part[half:]
    near, far = slice(0, 2 * PIECE), slice(2 * PIECE, 4 * PIECE)
    first = add_wide(first[near], swap_y(first[far])).astype(jnp.bfloat16)
    second = add_wide(second[near], swap_x(second[far])).astype(jnp.bfloat16)
    first = add_wide(first[:PIECE], swap_x(first[PIECE:]))
    second = add_wide(second[:PIECE], swap_y(second[PIECE:]))
    return jnp.concatenate([first, second], axis=0)


def reduce_rows(near_part, far_part):
    far_sum = reduce_side(far_part).astype(jnp.bfloat16)
    return add_wide(reduce_side(near_part), swap_zhi(far_sum))


def lane_tables(positions, width):
    lane = jnp.arange(width, dtype=jnp.int32) % HEAD_DIM
    half_rot = ROT // 2
    step = (lane % half_rot).astype(jnp.float32)
    inverse_freq = rope_base ** (-(step * (2.0 / ROT)))
    angles = positions.astype(jnp.float32)[:, None] * inverse_freq[None, :]
    sine = jnp.sin(angles)
    rotary = (lane < ROT)[None, :]
    low = (lane < half_rot)[None, :]
    cosine = jnp.where(rotary, jnp.cos(angles), 1.0)
    upper = jnp.where(rotary & ~low, sine, 0.0)
    lower = jnp.where(low, -sine, 0.0)
    return cosine, upper, lower


def project_kernel(rows_ref, weight_ref, bias_ref, cos_ref, up_ref, low_ref, keep_ref, send_ref):
    rows = rows_ref[...]
    for group in range(6):
        columns = slice(group * PAIR, (group + 1) * PAIR)
        part = jnp.dot(rows, weight_ref[:, columns], preferred_element_type=jnp.float32)
        part = part + bias_ref[:, columns]
        if group % 3 < 2:
            part = (
                part * cos_ref[...]
                + pltpu.roll(part, ROT // 2, 1) * up_ref[...]
                + pltpu.roll(part, PAIR - ROT // 2, 1) * low_ref[...]
            )
        target = keep_ref if group < 3 else send_ref
        spot = group % 3
        target[:, spot * PAIR : (spot + 1) * PAIR] = part.astype(jnp.bfloat16)


def project(rows, weight, bias, tables):
    count, width = rows.shape
    block = 256
    row_spec = pl.BlockSpec((block, width), lambda i: (i, 0))
    table_spec = pl.BlockSpec((block, PAIR), lambda i: (i, 0))
    out_spec = pl.BlockSpec((block, 3 * PAIR), lambda i: (i, 0))
    whole = lambda shape: pl.BlockSpec(shape, lambda i: (0, 0))
    out = jax.ShapeDtypeStruct((count, 3 * PAIR), jnp.bfloat16)
    return pl.pallas_call(
        project_kernel,
        grid=(count // block,),
        in_specs=[row_spec, whole(weight.shape), whole(bias.shape)] + [table_spec] * 3,
        out_specs=[out_spec, out_spec],
        out_shape=[out, out],
        cost_estimate=pl.CostEstimate(
            flops=2 * count * width * weight.shape[1],
            bytes_accessed=2 * (count * width + weight.size + count * weight.shape[1]),
            transcendentals=0,
        ),
        name="project",
    )(rows, weight, bias, *tables)


def attention_kernel(
    place_ref,
    mine_ref,
    their_ref,
    grad_mine_ref,
    grad_their_ref,
    cos_ref,
    up_ref,
    low_ref,
    out_mine_ref,
    out_their_ref,
    back_mine_ref,
    back_their_ref,
    head_q,
    head_k,
    head_v,
    head_g,
    out_all,
    back_all,
    grad_k,
    grad_v,
):
    which = pl.program_id(0)
    z_hi, z_lo, x_at = place_ref[0], place_ref[1], place_ref[2]
    scale = HEAD_DIM ** (-0.5)
    rows_all = head_k.shape[1]
    lane = lax.broadcasted_iota(jnp.int32, (1, PAIR), 1)
    in_head = [lane < HEAD_DIM, lane >= HEAD_DIM]

    def spots():
        for side in range(2):
            for half in range(2):
                for turn in range(2):
                    if half == 0:
                        piece = side * 8 + which * 2 + turn
                    else:
                        piece = side * 8 + 4 + turn * 2 + which
                    for other in range(2):
                        block = (z_hi ^ side) * 4 + (z_lo ^ other) * 2 + (x_at ^ turn)
                        start = pl.multiple_of(block * (2 * PIECE) + half * PIECE, PIECE)
                        yield piece, other, pl.ds(start, PIECE)

    for piece, other, rows in spots():
        source = (mine_ref, their_ref)[other]
        grad_source = (grad_mine_ref, grad_their_ref)[other]
        q_rows = source[piece, :, 0:PAIR] * jnp.bfloat16(scale)
        k_rows = source[piece, :, PAIR : 2 * PAIR]
        v_rows = source[piece, :, 2 * PAIR : 3 * PAIR]
        g_rows = grad_source[piece]
        zero = jnp.zeros_like(q_rows)
        for head in range(2):
            keep = in_head[head]
            head_q[head, rows, :] = jnp.where(keep, q_rows, zero)
            head_k[head, rows, :] = jnp.where(keep, k_rows, zero)
            head_v[head, rows, :] = jnp.where(keep, v_rows, zero)
            head_g[head, rows, :] = jnp.where(keep, g_rows, zero)

    grad_k[...] = jnp.zeros_like(grad_k)
    grad_v[...] = jnp.zeros_like(grad_v)
    by_rows = (((1,), (1,)), ((), ()))
    by_first = (((0,), (0,)), ((), ()))
    block = 256
    for at in range(rows_all // block):
        rows = slice(at * block, (at + 1) * block)
        count = (at + 1) * block
        keys = slice(0, count)
        query_at = at * block + lax.broadcasted_iota(jnp.int32, (block, count), 0)
        key_at = lax.broadcasted_iota(jnp.int32, (block, count), 1)
        allowed = key_at <= query_at
        out_rows = jnp.zeros((block, PAIR), jnp.float32)
        back_q = jnp.zeros((block, PAIR), jnp.float32)
        for head in range(2):
            q_rows = head_q[head, rows, :]
            g_rows = head_g[head, rows, :]
            k_rows = head_k[head, keys, :]
            v_rows = head_v[head, keys, :]
            scores = lax.dot_general(q_rows, k_rows, by_rows, preferred_element_type=jnp.float32)
            scores = jnp.where(allowed, scores, neg_large)
            peak = jnp.max(scores, axis=1, keepdims=True)
            weights = jnp.exp(scores - peak)
            total = jnp.sum(weights, axis=1, keepdims=True)
            weights = weights * (1.0 / total)
            narrow = weights.astype(jnp.bfloat16)
            out_head = jnp.dot(narrow, v_rows, preferred_element_type=jnp.float32)
            grad_weights = lax.dot_general(
                g_rows, v_rows, by_rows, preferred_element_type=jnp.float32
            )
            delta = jnp.sum(g_rows.astype(jnp.float32) * out_head, axis=1, keepdims=True)
            grad_scores = (weights * (grad_weights - delta)).astype(jnp.bfloat16)
            out_rows = out_rows + out_head
            back_q = back_q + jnp.dot(grad_scores, k_rows, preferred_element_type=jnp.float32)
            grad_k[keys, :] += lax.dot_general(
                grad_scores, q_rows, by_first, preferred_element_type=jnp.float32
            )
            grad_v[keys, :] += lax.dot_general(
                narrow, g_rows, by_first, preferred_element_type=jnp.float32
            )
        out_all[rows, :] = out_rows.astype(jnp.bfloat16)
        back_q = back_q * scale
        back_all[rows, 0:PAIR] = unroll_rotation(
            back_q, cos_ref[rows, :], up_ref[rows, :], low_ref[rows, :]
        )
    for at in range(rows_all // block):
        rows = slice(at * block, (at + 1) * block)
        back_all[rows, PAIR : 2 * PAIR] = unroll_rotation(
            grad_k[rows, :], cos_ref[rows, :], up_ref[rows, :], low_ref[rows, :]
        )
        back_all[rows, 2 * PAIR : 3 * PAIR] = grad_v[rows, :].astype(jnp.bfloat16)
    for piece, other, rows in spots():
        (out_mine_ref, out_their_ref)[other][piece] = out_all[rows, :]
        (back_mine_ref, back_their_ref)[other][piece] = back_all[rows, :]


def unroll_rotation(part, cosine, upper, lower):
    return (
        part * cosine
        - pltpu.roll(part, ROT // 2, 1) * upper
        - pltpu.roll(part, PAIR - ROT // 2, 1) * lower
    ).astype(jnp.bfloat16)


def attend(place, mine, their, grad_mine, grad_their, tables):
    rows = mine.shape[0]
    sequence = tables[0].shape[0]
    split = lambda a: a.reshape(PIECES, PIECE, a.shape[1])
    whole = lambda a: pl.BlockSpec(a.shape, lambda i, *_: (0,) * len(a.shape))
    args = [split(a) for a in (mine, their, grad_mine, grad_their)] + list(tables)
    outs = [jax.ShapeDtypeStruct(args[i].shape, jnp.bfloat16) for i in (2, 3, 0, 1)]
    head = pltpu.VMEM((2, sequence, PAIR), jnp.bfloat16)
    wide = pltpu.VMEM((sequence, PAIR), jnp.float32)
    pairs = 4 * sequence * sequence * 5 // 8
    results = pl.pallas_call(
        attention_kernel,
        grid_spec=pltpu.PrefetchScalarGridSpec(
            num_scalar_prefetch=1,
            grid=(2,),
            in_specs=[whole(a) for a in args],
            out_specs=[whole(a) for a in outs],
            scratch_shapes=[
                head,
                head,
                head,
                head,
                pltpu.VMEM((sequence, PAIR), jnp.bfloat16),
                pltpu.VMEM((sequence, 3 * PAIR), jnp.bfloat16),
                wide,
                wide,
            ],
        ),
        out_shape=outs,
        cost_estimate=pl.CostEstimate(
            flops=pairs * 6 * 2 * PAIR * 2, bytes_accessed=8 << 20, transcendentals=pairs
        ),
        name="attend",
    )(place, *args)
    return [a.reshape(rows, a.shape[2]) for a in results]


def by_sides(side_bit, own, other):
    return jnp.where(side_bit == 0, own, other), jnp.where(side_bit == 0, other, own)


def on_cycle(
    inputs, ln_gain, ln_bias, w_qkv, b_qkv, w_out, b_out, w_fc1, b_fc1, w_fc2, b_fc2, cotangent
):
    tokens = inputs[0].astype(jnp.float32)
    upstream = cotangent[0]
    token_count, model_width = tokens.shape
    both = ("ctx", "wa")
    devices = lax.axis_size("ctx") * lax.axis_size("wa")
    contract_rows = (((0,), (0,)), ((), ()))
    contract_cols = (((1,), (1,)), ((), ()))
    ctx_at, wa_at = lax.axis_index("ctx"), lax.axis_index("wa")
    z_hi, z_lo, x_at = ctx_at // 4, (ctx_at // 2) % 2, ctx_at % 2
    y_at, core = wa_at // 2, wa_at % 2
    quarter = z_hi * 2 + x_at
    own_pair = core ^ z_lo

    grad_rows = gather_rows(upstream)

    local_vectors = jnp.concatenate([ln_gain, ln_bias, b_qkv, b_out, b_fc2])
    vectors = lax.all_gather(local_vectors, "wa", axis=0)
    share = model_width // 4
    vector_parts = jnp.split(vectors, [share, 2 * share, 5 * share, 6 * share], axis=1)
    gain_all, shift_all, qkv_bias, out_bias, second_bias = [
        part.reshape(-1).astype(jnp.float32) for part in vector_parts
    ]
    centre = jnp.mean(tokens, axis=1, keepdims=True)
    centred = tokens - centre
    inverse = lax.rsqrt(jnp.mean(centred * centred, axis=1, keepdims=True) + eps_norm)
    scaled = centred * inverse
    normed_own = (scaled * gain_all + shift_all).astype(jnp.bfloat16)
    normed = gather_rows(normed_own)
    row_count = normed.shape[0]

    def unit_share(weight):
        units = weight.shape[0] // 4
        own = lax.dynamic_slice_in_dim(weight, quarter * units, units, 0)
        return jnp.concatenate([own, swap_core(own)], axis=0)

    qkv_view = w_qkv.reshape(share, 3, 2, 2, 4, PAIR)
    qkv_view = lax.dynamic_slice_in_dim(qkv_view, quarter, 1, 4)[:, :, :, :, 0]

    def pair_columns(y_side):
        part = lax.dynamic_slice_in_dim(qkv_view, y_side, 1, 2)[:, :, 0]
        first, second = by_sides(z_lo, part[:, :, 0], part[:, :, 1])
        return jnp.stack([first, second], axis=1).reshape(share, 6 * PAIR)

    own_rows = pair_columns(y_at)
    y_rows = swap_y(pair_columns(1 - y_at))
    chip_rows = jnp.stack(by_sides(y_at, own_rows, y_rows))
    core_rows = swap_core(chip_rows)
    qkv_weight = jnp.stack(by_sides(core, chip_rows, core_rows), axis=1).reshape(
        model_width, 6 * PAIR
    )
    bias_view = lax.dynamic_slice_in_dim(qkv_bias.reshape(3, 2, 2, 4, PAIR), y_at, 1, 1)
    bias_view = lax.dynamic_slice_in_dim(bias_view, quarter, 1, 3)[:, 0, :, 0]
    bias_pairs = jnp.stack(by_sides(z_lo, bias_view[:, 0], bias_view[:, 1]))
    qkv_bias_share = bias_pairs.reshape(1, 6 * PAIR)

    out_own = lax.dynamic_slice_in_dim(w_out, quarter * PAIR, PAIR, 0)
    out_weight = jnp.concatenate(by_sides(own_pair, out_own, swap_core(out_own)), axis=0)
    fc1_share, fc2_share = unit_share(w_fc1), unit_share(w_fc2)
    fc1_bias_share = unit_share(b_fc1).astype(jnp.float32)

    row_at = jnp.arange(row_count, dtype=jnp.int32)
    side, half, slot = row_at // 512, (row_at // 256) % 2, (row_at // PIECE) % 4
    turn = jnp.where(half == 0, slot % 2, slot // 2)
    block_at = (z_hi ^ side) * 4 + z_lo * 2 + (x_at ^ turn)
    positions = block_at * (2 * PIECE) + half * PIECE + row_at % PIECE
    tables_here = lane_tables(positions, PAIR)
    sequence = token_count * lax.axis_size("ctx")
    tables_all = lane_tables(jnp.arange(sequence, dtype=jnp.int32), PAIR)

    keep_heads, send_heads = project(normed, qkv_weight, qkv_bias_share, tables_here)
    their_heads = swap_zlo(send_heads)

    hidden = (
        lax.dot_general(normed, fc1_share, contract_cols, preferred_element_type=jnp.float32)
        + fc1_bias_share
    )
    gated = gelu_tanh(hidden).astype(jnp.bfloat16)

    grad_attended = lax.dot_general(
        grad_rows, out_weight, contract_cols, preferred_element_type=jnp.float32
    ).astype(jnp.bfloat16)
    their_grad = swap_zlo(grad_attended[:, PAIR:])
    place = jnp.stack([z_hi, z_lo, x_at]).astype(jnp.int32)
    out_mine, out_their, back_mine, back_their = attend(
        place, keep_heads, their_heads, grad_attended[:, :PAIR], their_grad, tables_all
    )
    attended = jnp.concatenate([out_mine, swap_zlo(out_their)], axis=1)
    grad_projected = jnp.concatenate([back_mine, swap_zlo(back_their)], axis=1)

    grad_gated = lax.dot_general(
        grad_rows, fc2_share, contract_cols, preferred_element_type=jnp.float32
    ).astype(jnp.bfloat16)
    ignored, slope_fn = jax.vjp(gelu_tanh, hidden)
    grad_hidden = slope_fn(grad_gated.astype(jnp.float32))[0].astype(jnp.bfloat16)
    units = fc1_share.shape[0] // 2

    def unit_grads(left, right):
        part = lax.dot_general(left, right, contract_rows, preferred_element_type=jnp.float32)
        part = add_wide(part[:units], swap_core(part[units:].astype(jnp.bfloat16)))
        part = part.astype(jnp.bfloat16).reshape(units, lax.axis_size("ctx"), -1)
        spread = lax.all_to_all(part.transpose(1, 0, 2), "ctx", 0, 0)
        spread = spread.reshape(2, 2, 2, units, -1)
        return add_wide(spread[:, 0], spread[:, 1]).reshape(4 * units, -1)

    grad_fc2 = unit_grads(gated, grad_rows)
    grad_fc1 = unit_grads(grad_hidden, normed)
    bias_sum = jnp.sum(grad_hidden.astype(jnp.float32), axis=0)
    bias_sum = bias_sum[:units] + swap_core(bias_sum[units:])
    bias_all = lax.all_gather(bias_sum, "ctx", axis=0).reshape(2, 2, 2, units)
    grad_b_fc1 = jnp.sum(bias_all, axis=1).reshape(4 * units)

    side_rows = row_count // 2

    def row_part(rows):
        return (
            jnp.dot(gated[rows], fc2_share, preferred_element_type=jnp.float32)
            + jnp.dot(attended[rows], out_weight, preferred_element_type=jnp.float32)
        ).astype(jnp.bfloat16)

    far_out, near_out = row_part(slice(side_rows, None)), row_part(slice(0, side_rows))
    outputs = (tokens + reduce_rows(near_out, far_out) + out_bias + second_bias).astype(
        jnp.bfloat16
    )[None]

    def grad_part(rows):
        return (
            jnp.dot(grad_hidden[rows], fc1_share, preferred_element_type=jnp.float32)
            + lax.dot_general(
                grad_projected[rows], qkv_weight, contract_cols, preferred_element_type=jnp.float32
            )
        ).astype(jnp.bfloat16)

    far_grad, near_grad = grad_part(slice(side_rows, None)), grad_part(slice(0, side_rows))
    grad_normed = reduce_rows(near_grad, far_grad)

    qkv_term = lax.dot_general(
        normed, grad_projected, contract_rows, preferred_element_type=jnp.float32
    )
    qkv_own = lax.dynamic_slice_in_dim(qkv_term, own_pair * 3 * PAIR, 3 * PAIR, 1)
    qkv_send = lax.dynamic_slice_in_dim(qkv_term, (1 - own_pair) * 3 * PAIR, 3 * PAIR, 1)
    qkv_own = add_wide(qkv_own, swap_core(qkv_send.astype(jnp.bfloat16))).astype(jnp.bfloat16)
    qkv_spread = lax.all_to_all(qkv_own, both, 0, 0, tiled=True)
    own_width = model_width // devices
    qkv_spread = qkv_spread.reshape(2, 2, 2, 2, 2, own_width, 3, PAIR)
    qkv_spread = add_wide(qkv_spread[:, 0], qkv_spread[:, 1])
    grad_qkv = qkv_spread.transpose(4, 5, 2, 3, 0, 1, 6).reshape(own_width, 3 * model_width)

    out_term = lax.dot_general(
        attended, grad_rows, contract_rows, preferred_element_type=jnp.float32
    )
    out_own_term = lax.dynamic_slice_in_dim(out_term, own_pair * PAIR, PAIR, 0)
    out_send = lax.dynamic_slice_in_dim(out_term, (1 - own_pair) * PAIR, PAIR, 0)
    out_own_term = add_wide(out_own_term, swap_core(out_send.astype(jnp.bfloat16)))
    head_keep = lax.dynamic_slice_in_dim(out_own_term, z_lo * HEAD_DIM, HEAD_DIM, 0)
    head_send = lax.dynamic_slice_in_dim(out_own_term, (1 - z_lo) * HEAD_DIM, HEAD_DIM, 0)
    head_sum = add_wide(head_keep, swap_zlo(head_send.astype(jnp.bfloat16)))
    routes = []
    for at in range(devices):
        bits = [(at >> shift) & 1 for shift in (4, 3, 2, 1, 0)]
        zh, zl, xx, yy, cc = bits
        routes.append((at, (((yy * 2 + cc) * 2 + zh) * 2 + xx) * 2 + zl))
    grad_out = lax.ppermute(head_sum.astype(jnp.bfloat16), both, routes).astype(jnp.float32)

    upstream_f32 = upstream.astype(jnp.float32)
    gain_term = jnp.sum(grad_normed * scaled, axis=0)
    shift_term = jnp.sum(grad_normed, axis=0)
    grad_scaled = grad_normed * gain_all
    grad_inputs = inverse * (
        grad_scaled
        - jnp.mean(grad_scaled, axis=1, keepdims=True)
        - scaled * jnp.mean(grad_scaled * scaled, axis=1, keepdims=True)
    )
    input_grads = (upstream_f32 + grad_inputs).astype(jnp.bfloat16)[None]

    pair_sums = jnp.sum(grad_projected.astype(jnp.float32), axis=0).reshape(2, 3, 1, PAIR)
    pair_sums = jnp.concatenate(by_sides(z_lo, pair_sums[0], pair_sums[1]), axis=1)
    in_y = (jnp.arange(2) == y_at).astype(jnp.float32)[None, :, None, None, None]
    in_quarter = (jnp.arange(4) == quarter).astype(jnp.float32)[None, None, None, :, None]
    qkv_sums = pair_sums[:, None, :, None, :] * in_y * in_quarter
    sums = jnp.concatenate(
        [
            gain_term.reshape(devices, -1),
            shift_term.reshape(devices, -1),
            jnp.sum(upstream_f32, axis=0).reshape(devices, -1),
            qkv_sums.reshape(devices, -1),
        ],
        axis=1,
    )
    sums = jnp.sum(lax.all_to_all(sums, both, 0, 0, tiled=True), axis=0)
    grad_ln_gain, grad_ln_bias, grad_b_out, grad_b_qkv = jnp.split(
        sums, [own_width, 2 * own_width, 3 * own_width]
    )
    return (
        outputs,
        input_grads,
        grad_ln_gain,
        grad_ln_bias,
        grad_qkv,
        grad_b_qkv,
        grad_out,
        grad_b_out,
        grad_fc1,
        grad_b_fc1,
        grad_fc2,
        grad_b_out,
    )


def solution(mesh):
    placed = (
        P("wa", "ctx", None),
        P("wa"),
        P("wa"),
        P("wa", None),
        P("wa"),
        P("wa", None),
        P("wa"),
        P("wa", None),
        P("wa"),
        P("wa", None),
        P("wa"),
        P("wa", "ctx", None),
    )

    def block(*arrays):
        rows = arrays[0].shape[1]
        on_cube = (mesh.shape["ctx"], mesh.shape["wa"], rows) == (8, 4, 2 * PIECE)
        return on_cycle(*arrays) if on_cube else on_device(*arrays)

    return jax.shard_map(
        block,
        mesh=mesh,
        in_specs=placed,
        out_specs=(
            P("wa", "ctx", None),
            P("wa", "ctx", None),
            P(("ctx", "wa")),
            P(("ctx", "wa")),
            P(("ctx", "wa"), None),
            P(("ctx", "wa")),
            P(("ctx", "wa"), None),
            P(("ctx", "wa")),
            P("wa", "ctx"),
            P("wa"),
            P("wa", "ctx"),
            P(("ctx", "wa")),
        ),
        check_vma=False,
    )
```

```python
import math

import jax
import jax.numpy as jnp
from jax import lax
from jax.experimental import pallas as pl
from jax.experimental.pallas import tpu as pltpu
from jax.sharding import PartitionSpec as P


HEADS = 32
HEAD_DIM = 64
ROT = 32


eps_norm = 1e-05
rope_base = 10000.0
key_block = 512
neg_large = -1e30
gelu_coeff = 0.7978845608028654


def gelu_tanh(pre_act):
    return (
        0.5
        * pre_act
        * (1.0 + jnp.tanh(gelu_coeff * (pre_act + 0.044715 * pre_act * pre_act * pre_act)))
    )


def rope_tables(positions):
    half_rot = ROT // 2
    inverse_freq = rope_base ** (-(jnp.arange(half_rot).astype(jnp.float32) * (2.0 / ROT)))
    angles = positions[:, None] * inverse_freq[None, :]
    angles = jnp.concatenate([angles, angles], axis=1)
    return (jnp.cos(angles), jnp.sin(angles))


def rotate(head_rows, cosine, sine_table):
    half_rot = ROT // 2
    rotary = head_rows[..., :ROT]
    turned = jnp.concatenate([-rotary[..., half_rot:], rotary[..., :half_rot]], axis=-1)
    rotary = rotary * cosine[:, None, :] + turned * sine_table[:, None, :]
    return jnp.concatenate([rotary, head_rows[..., ROT:]], axis=-1)


def unrotate(grad_rows, cosine, sine_table):
    half_rot = ROT // 2
    rotary = grad_rows[..., :ROT]
    moved = rotary * sine_table[:, None, :]
    turned = jnp.concatenate([moved[..., half_rot:], -moved[..., :half_rot]], axis=-1)
    rotary = rotary * cosine[:, None, :] + turned
    return jnp.concatenate([rotary, grad_rows[..., ROT:]], axis=-1)


def unchanged(current):
    return current


def on_device(
    inputs, ln_gain, ln_bias, w_qkv, b_qkv, w_out, b_out, w_fc1, b_fc1, w_fc2, b_fc2, cotangent
):
    tokens = inputs[0].astype(jnp.float32)
    token_count, model_width = tokens.shape
    contract_rows = (((0,), (0,)), ((), ()))
    contract_cols = (((1,), (1,)), ((), ()))
    gain_all, shift_all, qkv_weight, qkv_bias, out_weight, out_bias, second_bias = (
        lax.all_gather(ln_gain, "wa", axis=0, tiled=True),
        lax.all_gather(ln_bias, "wa", axis=0, tiled=True),
        lax.all_gather(w_qkv, "wa", axis=0, tiled=True),
        lax.all_gather(b_qkv, "wa", axis=0, tiled=True),
        lax.all_gather(w_out, "wa", axis=0, tiled=True),
        lax.all_gather(b_out, "wa", axis=0, tiled=True),
        lax.all_gather(b_fc2, "wa", axis=0, tiled=True),
    )
    centre = jnp.mean(tokens, axis=1, keepdims=True)
    centred = tokens - centre
    inverse = lax.rsqrt(jnp.mean(centred * centred, axis=1, keepdims=True) + eps_norm)
    scaled = centred * inverse
    normed = (scaled * gain_all + shift_all).astype(jnp.bfloat16)
    projected = jnp.dot(normed, qkv_weight, preferred_element_type=jnp.float32) + qkv_bias
    offset = lax.axis_index("ctx") * token_count
    query_pos = offset + jnp.arange(token_count, dtype=jnp.int32)
    last_query = offset + token_count - 1
    cosine, sine_table = rope_tables(query_pos.astype(jnp.float32))
    head_shape = (token_count, HEADS, HEAD_DIM)
    queries = rotate(projected[:, :model_width].reshape(head_shape), cosine, sine_table).astype(
        jnp.bfloat16
    )
    key_rows = (
        rotate(projected[:, model_width : 2 * model_width].reshape(head_shape), cosine, sine_table)
        .astype(jnp.bfloat16)
        .reshape(token_count, model_width)
    )
    value_rows = projected[:, 2 * model_width :].astype(jnp.bfloat16)
    score_scale = HEAD_DIM ** (-0.5)
    start_state = (
        jnp.full((HEADS, token_count), neg_large, jnp.float32),
        jnp.zeros((HEADS, token_count), jnp.float32),
        jnp.zeros((token_count, HEADS, HEAD_DIM), jnp.float32),
    )
    running = start_state
    key_part = lax.all_gather(key_rows, "ctx", axis=0, tiled=True)
    value_part = lax.all_gather(value_rows, "ctx", axis=0, tiled=True)
    row_count = key_part.shape[0]
    block_rows = math.gcd(row_count, key_block)
    block_count = row_count // block_rows
    key_blocks = key_part.reshape(block_count, block_rows, HEADS, HEAD_DIM)
    value_blocks = value_part.reshape(block_count, block_rows, HEADS, HEAD_DIM)

    def visit_block(current, block_items):
        block_index, key_slab, value_slab = block_items
        start_row = block_index * block_rows

        def attend(state_now):
            row_peak, row_total, weighted = state_now
            raw_scores = jnp.einsum(
                "qhd,khd->hqk", queries, key_slab, preferred_element_type=jnp.float32
            )
            key_pos = start_row + jnp.arange(block_rows, dtype=jnp.int32)
            allowed = (key_pos[None, :] <= query_pos[:, None])[None]
            scores = jnp.where(allowed, raw_scores * score_scale, neg_large)
            new_peak = jnp.maximum(row_peak, jnp.max(scores, axis=2))
            factor = jnp.exp(row_peak - new_peak)
            exp_scores = jnp.where(allowed, jnp.exp(scores - new_peak[:, :, None]), 0.0)
            row_total = row_total * factor + jnp.sum(exp_scores, axis=2)
            weighted = weighted * jnp.transpose(factor)[:, :, None] + jnp.einsum(
                "hqk,khd->qhd",
                exp_scores.astype(jnp.bfloat16),
                value_slab,
                preferred_element_type=jnp.float32,
            )
            return (new_peak, row_total, weighted)

        return (lax.cond(start_row <= last_query, attend, unchanged, current), None)

    running, ignored = lax.scan(
        visit_block, running, (jnp.arange(block_count, dtype=jnp.int32), key_blocks, value_blocks)
    )
    row_peak, row_total, weighted = running
    log_total = row_peak + jnp.log(row_total)
    attended_f32 = weighted / jnp.transpose(row_total)[:, :, None]
    attended = attended_f32.reshape(token_count, model_width).astype(jnp.bfloat16)
    branch_attn = jnp.dot(attended, out_weight, preferred_element_type=jnp.float32) + out_bias
    upstream = cotangent[0]
    upstream_f32 = upstream.astype(jnp.float32)
    fc1_all, fc1_bias_all, fc2_all = (
        lax.all_gather(w_fc1, "wa", axis=0, tiled=True),
        lax.all_gather(b_fc1, "wa", axis=0, tiled=True),
        lax.all_gather(w_fc2, "wa", axis=0, tiled=True),
    )
    hidden = (
        lax.dot_general(normed, fc1_all, contract_cols, preferred_element_type=jnp.float32)
        + fc1_bias_all
    )
    gated_act = gelu_tanh(hidden).astype(jnp.bfloat16)
    branch_mlp = jnp.dot(gated_act, fc2_all, preferred_element_type=jnp.float32) + second_bias
    outputs = (tokens + branch_attn + branch_mlp).astype(jnp.bfloat16)[None]
    grad_gated = lax.dot_general(
        upstream, fc2_all, contract_cols, preferred_element_type=jnp.float32
    ).astype(jnp.bfloat16)
    fc2_term = lax.dot_general(
        gated_act, upstream, contract_rows, preferred_element_type=jnp.float32
    )
    ignored, slope_fn = jax.vjp(gelu_tanh, hidden)
    grad_hidden = slope_fn(grad_gated.astype(jnp.float32))[0].astype(jnp.bfloat16)
    fc1_bias_term = jnp.sum(grad_hidden.astype(jnp.float32), axis=0)
    fc1_term = lax.dot_general(
        grad_hidden, normed, contract_rows, preferred_element_type=jnp.float32
    )
    grad_normed_mlp = jnp.dot(grad_hidden, fc1_all, preferred_element_type=jnp.float32)
    fc1_share, fc2_share, bias_share = (
        lax.psum_scatter(
            fc1_term.astype(jnp.bfloat16), "wa", scatter_dimension=0, tiled=True
        ).astype(jnp.float32),
        lax.psum_scatter(
            fc2_term.astype(jnp.bfloat16), "wa", scatter_dimension=0, tiled=True
        ).astype(jnp.float32),
        lax.psum_scatter(
            fc1_bias_term.astype(jnp.bfloat16), "wa", scatter_dimension=0, tiled=True
        ).astype(jnp.float32),
    )
    grad_fc1, grad_fc2 = (
        lax.psum_scatter(
            fc1_share.astype(jnp.bfloat16), "ctx", scatter_dimension=1, tiled=True
        ).astype(jnp.float32),
        lax.psum_scatter(
            fc2_share.astype(jnp.bfloat16), "ctx", scatter_dimension=1, tiled=True
        ).astype(jnp.float32),
    )
    grad_b_fc1 = lax.psum(bias_share, "ctx")
    out_term = lax.dot_general(
        attended, upstream, contract_rows, preferred_element_type=jnp.float32
    )
    bias_term = jnp.sum(upstream_f32, axis=0)
    grad_attended = (
        lax.dot_general(upstream, out_weight, contract_cols, preferred_element_type=jnp.float32)
        .astype(jnp.bfloat16)
        .reshape(head_shape)
    )
    row_deltas = jnp.transpose(jnp.sum(grad_attended.astype(jnp.float32) * attended_f32, axis=2))
    keys_all, values_all = (
        lax.all_gather(key_rows, "ctx", axis=0, tiled=True),
        lax.all_gather(value_rows, "ctx", axis=0, tiled=True),
    )
    sequence_rows = keys_all.shape[0]

    def block_scores(key_slab, value_slab, start_row, block_rows):
        raw_scores = jnp.einsum(
            "qhd,khd->hqk", queries, key_slab, preferred_element_type=jnp.float32
        )
        key_pos = start_row + jnp.arange(block_rows, dtype=jnp.int32)
        allowed = (key_pos[None, :] <= query_pos[:, None])[None]
        probabilities = jnp.where(
            allowed, jnp.exp(raw_scores * score_scale - log_total[:, :, None]), 0.0
        )
        grad_probs = jnp.einsum(
            "qhd,khd->hqk", grad_attended, value_slab, preferred_element_type=jnp.float32
        )
        grad_raw = (probabilities * (grad_probs - row_deltas[:, :, None]) * score_scale).astype(
            jnp.bfloat16
        )
        return (probabilities, grad_raw)

    def slabs_at(start_row, block_rows):
        key_slab = lax.dynamic_slice_in_dim(keys_all, start_row, block_rows, 0).reshape(
            block_rows, HEADS, HEAD_DIM
        )
        value_slab = lax.dynamic_slice_in_dim(values_all, start_row, block_rows, 0).reshape(
            block_rows, HEADS, HEAD_DIM
        )
        return (key_slab, value_slab)

    query_block_rows = math.gcd(sequence_rows, key_block)

    def query_visit(grad_queries, block_index):
        start_row = block_index * query_block_rows

        def accumulate(current):
            key_slab, value_slab = slabs_at(start_row, query_block_rows)
            _, grad_raw = block_scores(key_slab, value_slab, start_row, query_block_rows)
            return current + jnp.einsum(
                "hqk,khd->qhd", grad_raw, key_slab, preferred_element_type=jnp.float32
            )

        return (lax.cond(start_row <= last_query, accumulate, unchanged, grad_queries), None)

    grad_queries, ignored = lax.scan(
        query_visit,
        jnp.zeros(head_shape, jnp.float32),
        jnp.arange(sequence_rows // query_block_rows, dtype=jnp.int32),
    )
    row_count = lax.axis_size("ctx") * token_count
    key_block_rows = math.gcd(row_count, key_block)

    def term_visit(dummy, block_index):
        start_row = block_index * key_block_rows

        def contribute(operand):
            key_slab, value_slab = slabs_at(start_row, key_block_rows)
            probabilities, grad_raw = block_scores(key_slab, value_slab, start_row, key_block_rows)
            grad_key_slab = jnp.einsum(
                "hqk,qhd->khd", grad_raw, queries, preferred_element_type=jnp.float32
            ).reshape(key_block_rows, model_width)
            grad_value_slab = jnp.einsum(
                "hqk,qhd->khd",
                probabilities.astype(jnp.bfloat16),
                grad_attended,
                preferred_element_type=jnp.float32,
            ).reshape(key_block_rows, model_width)
            return jnp.concatenate([grad_key_slab, grad_value_slab], axis=1)

        def nothing(operand):
            return jnp.zeros((key_block_rows, 2 * model_width), jnp.float32)

        return (dummy, lax.cond(start_row <= last_query, contribute, nothing, 0))

    _, stacked = lax.scan(term_visit, 0, jnp.arange(row_count // key_block_rows, dtype=jnp.int32))
    key_grads = lax.psum_scatter(
        stacked.reshape(row_count, 2 * model_width).astype(jnp.bfloat16),
        "ctx",
        scatter_dimension=0,
        tiled=True,
    ).astype(jnp.float32)
    grad_keys = unrotate(
        key_grads[:, :model_width].reshape(head_shape), cosine, sine_table
    ).reshape(token_count, model_width)
    grad_values = key_grads[:, model_width:]
    grad_query_pre = unrotate(grad_queries, cosine, sine_table).reshape(token_count, model_width)
    grad_projected = jnp.concatenate([grad_query_pre, grad_keys, grad_values], axis=1).astype(
        jnp.bfloat16
    )
    qkv_term = lax.dot_general(
        normed, grad_projected, contract_rows, preferred_element_type=jnp.float32
    )
    qkv_bias_term = jnp.sum(grad_projected.astype(jnp.float32), axis=0)
    grad_normed = (
        lax.dot_general(
            grad_projected, qkv_weight, contract_cols, preferred_element_type=jnp.float32
        )
        + grad_normed_mlp
    )
    gain_term = jnp.sum(grad_normed * scaled, axis=0)
    shift_term = jnp.sum(grad_normed, axis=0)
    grad_scaled = grad_normed * gain_all
    grad_inputs = inverse * (
        grad_scaled
        - jnp.mean(grad_scaled, axis=1, keepdims=True)
        - scaled * jnp.mean(grad_scaled * scaled, axis=1, keepdims=True)
    )
    input_grads = (upstream_f32 + grad_inputs).astype(jnp.bfloat16)[None]
    grad_ln_gain, grad_ln_bias, grad_qkv, grad_b_qkv, grad_out, grad_b_out = (
        lax.psum_scatter(gain_term, ("ctx", "wa"), scatter_dimension=0, tiled=True),
        lax.psum_scatter(shift_term, ("ctx", "wa"), scatter_dimension=0, tiled=True),
        lax.psum_scatter(qkv_term, ("ctx", "wa"), scatter_dimension=0, tiled=True),
        lax.psum_scatter(qkv_bias_term, ("ctx", "wa"), scatter_dimension=0, tiled=True),
        lax.psum_scatter(out_term, ("ctx", "wa"), scatter_dimension=0, tiled=True),
        lax.psum_scatter(bias_term, ("ctx", "wa"), scatter_dimension=0, tiled=True),
    )
    return (
        outputs,
        input_grads,
        grad_ln_gain,
        grad_ln_bias,
        grad_qkv,
        grad_b_qkv,
        grad_out,
        grad_b_out,
        grad_fc1,
        grad_b_fc1,
        grad_fc2,
        grad_b_out,
    )


def swap(values, axis, bit):
    return lax.ppermute(values, axis, [(at, at ^ bit) for at in range(lax.axis_size(axis))])


X_BIT, ZLO_BIT, ZHI_BIT = 1, 2, 4
CORE_BIT, Y_BIT = 1, 2
PIECE = 64
PIECES = 16
PAIR = 2 * HEAD_DIM


def swap_x(values):
    return swap(values, "ctx", X_BIT)


def swap_y(values):
    return swap(values, "wa", Y_BIT)


def swap_zhi(values):
    return swap(values, "ctx", ZHI_BIT)


def swap_zlo(values):
    return swap(values, "ctx", ZLO_BIT)


def swap_core(values):
    return swap(values, "wa", CORE_BIT)


def gather_rows(block):
    sides = (block, swap_zhi(block))
    pieces = []
    for side in sides:
        first, second = side[:PIECE], side[PIECE:]
        first_x = swap_x(first)
        second_y = swap_y(second)
        first_y = swap_y(first)
        second_x = swap_x(second)
        first_xy = swap_y(first_x)
        second_xy = swap_x(second_y)
        pieces += [first, first_x, first_y, first_xy, second, second_y, second_x, second_xy]
    return jnp.concatenate(pieces, axis=0)


def add_wide(mine, other):
    return mine.astype(jnp.float32) + other.astype(jnp.float32)


def reduce_side(part):
    half = 4 * PIECE
    first, second = part[:half], part[half:]
    near, far = slice(0, 2 * PIECE), slice(2 * PIECE, 4 * PIECE)
    first = add_wide(first[near], swap_y(first[far])).astype(jnp.bfloat16)
    second = add_wide(second[near], swap_x(second[far])).astype(jnp.bfloat16)
    first = add_wide(first[:PIECE], swap_x(first[PIECE:]))
    second = add_wide(second[:PIECE], swap_y(second[PIECE:]))
    return jnp.concatenate([first, second], axis=0)


def reduce_rows(near_part, far_part):
    far_sum = reduce_side(far_part).astype(jnp.bfloat16)
    return add_wide(reduce_side(near_part), swap_zhi(far_sum))


def lane_tables(positions, width):
    lane = jnp.arange(width, dtype=jnp.int32) % HEAD_DIM
    half_rot = ROT // 2
    step = (lane % half_rot).astype(jnp.float32)
    inverse_freq = rope_base ** (-(step * (2.0 / ROT)))
    angles = positions.astype(jnp.float32)[:, None] * inverse_freq[None, :]
    sine = jnp.sin(angles)
    rotary = (lane < ROT)[None, :]
    low = (lane < half_rot)[None, :]
    cosine = jnp.where(rotary, jnp.cos(angles), 1.0)
    upper = jnp.where(rotary & ~low, sine, 0.0)
    lower = jnp.where(low, -sine, 0.0)
    return cosine, upper, lower


def project_kernel(rows_ref, weight_ref, bias_ref, cos_ref, up_ref, low_ref, keep_ref, send_ref):
    rows = rows_ref[...]
    for group in range(6):
        columns = slice(group * PAIR, (group + 1) * PAIR)
        part = jnp.dot(rows, weight_ref[:, columns], preferred_element_type=jnp.float32)
        part = part + bias_ref[:, columns]
        if group % 3 < 2:
            part = (
                part * cos_ref[...]
                + pltpu.roll(part, ROT // 2, 1) * up_ref[...]
                + pltpu.roll(part, PAIR - ROT // 2, 1) * low_ref[...]
            )
        target = keep_ref if group < 3 else send_ref
        spot = group % 3
        target[:, spot * PAIR : (spot + 1) * PAIR] = part.astype(jnp.bfloat16)


def project(rows, weight, bias, tables):
    count, width = rows.shape
    block = 256
    row_spec = pl.BlockSpec((block, width), lambda i: (i, 0))
    table_spec = pl.BlockSpec((block, PAIR), lambda i: (i, 0))
    out_spec = pl.BlockSpec((block, 3 * PAIR), lambda i: (i, 0))
    whole = lambda shape: pl.BlockSpec(shape, lambda i: (0, 0))
    out = jax.ShapeDtypeStruct((count, 3 * PAIR), jnp.bfloat16)
    return pl.pallas_call(
        project_kernel,
        grid=(count // block,),
        in_specs=[row_spec, whole(weight.shape), whole(bias.shape)] + [table_spec] * 3,
        out_specs=[out_spec, out_spec],
        out_shape=[out, out],
        cost_estimate=pl.CostEstimate(
            flops=2 * count * width * weight.shape[1],
            bytes_accessed=2 * (count * width + weight.size + count * weight.shape[1]),
            transcendentals=0,
        ),
        name="project",
    )(rows, weight, bias, *tables)


def attention_kernel(
    place_ref,
    mine_ref,
    their_ref,
    grad_mine_ref,
    grad_their_ref,
    cos_ref,
    up_ref,
    low_ref,
    out_mine_ref,
    out_their_ref,
    back_mine_ref,
    back_their_ref,
    head_q,
    head_k,
    head_v,
    head_g,
    out_all,
    back_all,
    grad_k,
    grad_v,
):
    which = pl.program_id(0)
    z_hi, z_lo, x_at = place_ref[0], place_ref[1], place_ref[2]
    scale = HEAD_DIM ** (-0.5)
    rows_all = head_k.shape[1]
    lane = lax.broadcasted_iota(jnp.int32, (1, PAIR), 1)
    in_head = [lane < HEAD_DIM, lane >= HEAD_DIM]

    def spots():
        for side in range(2):
            for half in range(2):
                for turn in range(2):
                    if half == 0:
                        piece = side * 8 + which * 2 + turn
                    else:
                        piece = side * 8 + 4 + turn * 2 + which
                    for other in range(2):
                        block = (z_hi ^ side) * 4 + (z_lo ^ other) * 2 + (x_at ^ turn)
                        start = pl.multiple_of(block * (2 * PIECE) + half * PIECE, PIECE)
                        yield piece, other, pl.ds(start, PIECE)

    for piece, other, rows in spots():
        source = (mine_ref, their_ref)[other]
        grad_source = (grad_mine_ref, grad_their_ref)[other]
        q_rows = source[piece, :, 0:PAIR] * jnp.bfloat16(scale)
        k_rows = source[piece, :, PAIR : 2 * PAIR]
        v_rows = source[piece, :, 2 * PAIR : 3 * PAIR]
        g_rows = grad_source[piece]
        zero = jnp.zeros_like(q_rows)
        for head in range(2):
            keep = in_head[head]
            head_q[head, rows, :] = jnp.where(keep, q_rows, zero)
            head_k[head, rows, :] = jnp.where(keep, k_rows, zero)
            head_v[head, rows, :] = jnp.where(keep, v_rows, zero)
            head_g[head, rows, :] = jnp.where(keep, g_rows, zero)

    grad_k[...] = jnp.zeros_like(grad_k)
    grad_v[...] = jnp.zeros_like(grad_v)
    by_rows = (((1,), (1,)), ((), ()))
    by_first = (((0,), (0,)), ((), ()))
    block = 256
    for at in range(rows_all // block):
        rows = slice(at * block, (at + 1) * block)
        count = (at + 1) * block
        keys = slice(0, count)
        query_at = at * block + lax.broadcasted_iota(jnp.int32, (block, count), 0)
        key_at = lax.broadcasted_iota(jnp.int32, (block, count), 1)
        allowed = key_at <= query_at
        out_rows = jnp.zeros((block, PAIR), jnp.float32)
        back_q = jnp.zeros((block, PAIR), jnp.float32)
        for head in range(2):
            q_rows = head_q[head, rows, :]
            g_rows = head_g[head, rows, :]
            k_rows = head_k[head, keys, :]
            v_rows = head_v[head, keys, :]
            scores = lax.dot_general(q_rows, k_rows, by_rows, preferred_element_type=jnp.float32)
            scores = jnp.where(allowed, scores, neg_large)
            peak = jnp.max(scores, axis=1, keepdims=True)
            weights = jnp.exp(scores - peak)
            total = jnp.sum(weights, axis=1, keepdims=True)
            weights = weights * (1.0 / total)
            narrow = weights.astype(jnp.bfloat16)
            out_head = jnp.dot(narrow, v_rows, preferred_element_type=jnp.float32)
            grad_weights = lax.dot_general(
                g_rows, v_rows, by_rows, preferred_element_type=jnp.float32
            )
            delta = jnp.sum(g_rows.astype(jnp.float32) * out_head, axis=1, keepdims=True)
            grad_scores = (weights * (grad_weights - delta)).astype(jnp.bfloat16)
            out_rows = out_rows + out_head
            back_q = back_q + jnp.dot(grad_scores, k_rows, preferred_element_type=jnp.float32)
            grad_k[keys, :] += lax.dot_general(
                grad_scores, q_rows, by_first, preferred_element_type=jnp.float32
            )
            grad_v[keys, :] += lax.dot_general(
                narrow, g_rows, by_first, preferred_element_type=jnp.float32
            )
        out_all[rows, :] = out_rows.astype(jnp.bfloat16)
        back_q = back_q * scale
        back_all[rows, 0:PAIR] = unroll_rotation(
            back_q, cos_ref[rows, :], up_ref[rows, :], low_ref[rows, :]
        )
    for at in range(rows_all // block):
        rows = slice(at * block, (at + 1) * block)
        back_all[rows, PAIR : 2 * PAIR] = unroll_rotation(
            grad_k[rows, :], cos_ref[rows, :], up_ref[rows, :], low_ref[rows, :]
        )
        back_all[rows, 2 * PAIR : 3 * PAIR] = grad_v[rows, :].astype(jnp.bfloat16)
    for piece, other, rows in spots():
        (out_mine_ref, out_their_ref)[other][piece] = out_all[rows, :]
        (back_mine_ref, back_their_ref)[other][piece] = back_all[rows, :]


def unroll_rotation(part, cosine, upper, lower):
    return (
        part * cosine
        - pltpu.roll(part, ROT // 2, 1) * upper
        - pltpu.roll(part, PAIR - ROT // 2, 1) * lower
    ).astype(jnp.bfloat16)


def attend(place, mine, their, grad_mine, grad_their, tables):
    rows = mine.shape[0]
    sequence = tables[0].shape[0]
    split = lambda a: a.reshape(PIECES, PIECE, a.shape[1])
    whole = lambda a: pl.BlockSpec(a.shape, lambda i, *_: (0,) * len(a.shape))
    args = [split(a) for a in (mine, their, grad_mine, grad_their)] + list(tables)
    outs = [jax.ShapeDtypeStruct(args[i].shape, jnp.bfloat16) for i in (2, 3, 0, 1)]
    head = pltpu.VMEM((2, sequence, PAIR), jnp.bfloat16)
    wide = pltpu.VMEM((sequence, PAIR), jnp.float32)
    pairs = 4 * sequence * sequence * 5 // 8
    results = pl.pallas_call(
        attention_kernel,
        grid_spec=pltpu.PrefetchScalarGridSpec(
            num_scalar_prefetch=1,
            grid=(2,),
            in_specs=[whole(a) for a in args],
            out_specs=[whole(a) for a in outs],
            scratch_shapes=[
                head,
                head,
                head,
                head,
                pltpu.VMEM((sequence, PAIR), jnp.bfloat16),
                pltpu.VMEM((sequence, 3 * PAIR), jnp.bfloat16),
                wide,
                wide,
            ],
        ),
        out_shape=outs,
        cost_estimate=pl.CostEstimate(
            flops=pairs * 6 * 2 * PAIR * 2, bytes_accessed=8 << 20, transcendentals=pairs
        ),
        name="attend",
    )(place, *args)
    return [a.reshape(rows, a.shape[2]) for a in results]


def by_sides(side_bit, own, other):
    return jnp.where(side_bit == 0, own, other), jnp.where(side_bit == 0, other, own)


def on_cycle(
    inputs, ln_gain, ln_bias, w_qkv, b_qkv, w_out, b_out, w_fc1, b_fc1, w_fc2, b_fc2, cotangent
):
    tokens = inputs[0].astype(jnp.float32)
    upstream = cotangent[0]
    token_count, model_width = tokens.shape
    both = ("ctx", "wa")
    devices = lax.axis_size("ctx") * lax.axis_size("wa")
    contract_rows = (((0,), (0,)), ((), ()))
    contract_cols = (((1,), (1,)), ((), ()))
    ctx_at, wa_at = lax.axis_index("ctx"), lax.axis_index("wa")
    z_hi, z_lo, x_at = ctx_at // 4, (ctx_at // 2) % 2, ctx_at % 2
    y_at, core = wa_at // 2, wa_at % 2
    quarter = z_hi * 2 + x_at
    own_pair = core ^ z_lo

    grad_rows = gather_rows(upstream)

    local_vectors = jnp.concatenate([ln_gain, ln_bias, b_qkv, b_out, b_fc2])
    vectors = lax.all_gather(local_vectors, "wa", axis=0)
    share = model_width // 4
    vector_parts = jnp.split(vectors, [share, 2 * share, 5 * share, 6 * share], axis=1)
    gain_all, shift_all, qkv_bias, out_bias, second_bias = [
        part.reshape(-1).astype(jnp.float32) for part in vector_parts
    ]
    centre = jnp.mean(tokens, axis=1, keepdims=True)
    centred = tokens - centre
    inverse = lax.rsqrt(jnp.mean(centred * centred, axis=1, keepdims=True) + eps_norm)
    scaled = centred * inverse
    normed_own = (scaled * gain_all + shift_all).astype(jnp.bfloat16)
    normed = gather_rows(normed_own)
    row_count = normed.shape[0]

    def unit_share(weight):
        units = weight.shape[0] // 4
        own = lax.dynamic_slice_in_dim(weight, quarter * units, units, 0)
        return jnp.concatenate([own, swap_core(own)], axis=0)

    qkv_view = w_qkv.reshape(share, 3, 2, 2, 4, PAIR)
    qkv_view = lax.dynamic_slice_in_dim(qkv_view, quarter, 1, 4)[:, :, :, :, 0]

    def pair_columns(y_side):
        part = lax.dynamic_slice_in_dim(qkv_view, y_side, 1, 2)[:, :, 0]
        first, second = by_sides(z_lo, part[:, :, 0], part[:, :, 1])
        return jnp.stack([first, second], axis=1).reshape(share, 6 * PAIR)

    own_rows = pair_columns(y_at)
    y_rows = swap_y(pair_columns(1 - y_at))
    chip_rows = jnp.stack(by_sides(y_at, own_rows, y_rows))
    core_rows = swap_core(chip_rows)
    qkv_weight = jnp.stack(by_sides(core, chip_rows, core_rows), axis=1).reshape(
        model_width, 6 * PAIR
    )
    bias_view = lax.dynamic_slice_in_dim(qkv_bias.reshape(3, 2, 2, 4, PAIR), y_at, 1, 1)
    bias_view = lax.dynamic_slice_in_dim(bias_view, quarter, 1, 3)[:, 0, :, 0]
    bias_pairs = jnp.stack(by_sides(z_lo, bias_view[:, 0], bias_view[:, 1]))
    qkv_bias_share = bias_pairs.reshape(1, 6 * PAIR)

    out_own = lax.dynamic_slice_in_dim(w_out, quarter * PAIR, PAIR, 0)
    out_weight = jnp.concatenate(by_sides(own_pair, out_own, swap_core(out_own)), axis=0)
    fc1_share, fc2_share = unit_share(w_fc1), unit_share(w_fc2)
    fc1_bias_share = unit_share(b_fc1).astype(jnp.float32)

    row_at = jnp.arange(row_count, dtype=jnp.int32)
    side, half, slot = row_at // 512, (row_at // 256) % 2, (row_at // PIECE) % 4
    turn = jnp.where(half == 0, slot % 2, slot // 2)
    block_at = (z_hi ^ side) * 4 + z_lo * 2 + (x_at ^ turn)
    positions = block_at * (2 * PIECE) + half * PIECE + row_at % PIECE
    tables_here = lane_tables(positions, PAIR)
    sequence = token_count * lax.axis_size("ctx")
    tables_all = lane_tables(jnp.arange(sequence, dtype=jnp.int32), PAIR)

    keep_heads, send_heads = project(normed, qkv_weight, qkv_bias_share, tables_here)
    their_heads = swap_zlo(send_heads)

    hidden = (
        lax.dot_general(normed, fc1_share, contract_cols, preferred_element_type=jnp.float32)
        + fc1_bias_share
    )
    gated = gelu_tanh(hidden).astype(jnp.bfloat16)

    grad_attended = lax.dot_general(
        grad_rows, out_weight, contract_cols, preferred_element_type=jnp.float32
    ).astype(jnp.bfloat16)
    their_grad = swap_zlo(grad_attended[:, PAIR:])
    place = jnp.stack([z_hi, z_lo, x_at]).astype(jnp.int32)
    out_mine, out_their, back_mine, back_their = attend(
        place, keep_heads, their_heads, grad_attended[:, :PAIR], their_grad, tables_all
    )
    attended = jnp.concatenate([out_mine, swap_zlo(out_their)], axis=1)
    back_returned = swap_zlo(back_their)
    grad_projected = jnp.concatenate([back_mine, back_returned], axis=1)

    rows_late, ignored = lax.optimization_barrier((grad_rows, out_mine))
    grad_gated = lax.dot_general(
        rows_late, fc2_share, contract_cols, preferred_element_type=jnp.float32
    ).astype(jnp.bfloat16)
    ignored, slope_fn = jax.vjp(gelu_tanh, hidden)
    grad_hidden = slope_fn(grad_gated.astype(jnp.float32))[0].astype(jnp.bfloat16)
    bias_sum = jnp.sum(grad_hidden.astype(jnp.float32), axis=0)
    units = fc1_share.shape[0] // 2

    def to_owner(values, dz, dx):
        return swap(values, "ctx", dz * ZHI_BIT + dx * X_BIT) if dz or dx else values

    def spread_over_cycle(total, axis):
        size = total.shape[axis]
        take = lambda a, start, count: lax.dynamic_slice_in_dim(a, start, count, axis)
        parts = {}
        for dz in (1, 0):
            side_start = (z_hi ^ dz) * (size // 2)
            send = take(total, side_start + (1 - z_lo) * (size // 4), size // 4)
            keep = take(total, side_start + z_lo * (size // 4), size // 4)
            received = swap_zlo(send)
            both_sum = add_wide(keep, received).astype(jnp.bfloat16)
            for dx in (1, 0):
                piece = take(both_sum, (x_at ^ dx) * (size // 8), size // 8)
                parts[dz, dx] = to_owner(piece, dz, dx)
        near = by_sides(x_at, parts[0, 0], parts[0, 1])
        far = by_sides(x_at, parts[1, 0], parts[1, 1])
        x_low = by_sides(z_hi, near[0], far[0])
        x_high = by_sides(z_hi, near[1], far[1])
        return [x_low[0], x_high[0], x_low[1], x_high[1]]

    def unit_grads(left, right):
        grad_of = lambda a: lax.dot_general(
            a, right, contract_rows, preferred_element_type=jnp.float32
        ).astype(jnp.bfloat16)
        theirs = grad_of(left[:, units:])
        theirs = swap_core(theirs)
        total = add_wide(grad_of(left[:, :units]), theirs).astype(jnp.bfloat16)
        return jnp.concatenate(spread_over_cycle(total, 1), axis=0).astype(jnp.float32)

    grad_fc2 = unit_grads(gated, grad_rows)
    grad_fc1 = unit_grads(grad_hidden, normed)
    bias_sum = bias_sum[:units] + swap_core(bias_sum[units:])
    bias_sum = bias_sum + swap_zlo(bias_sum)
    bias_sum = jnp.concatenate(by_sides(x_at, bias_sum, swap_x(bias_sum)))
    grad_b_fc1 = jnp.concatenate(by_sides(z_hi, bias_sum, swap_zhi(bias_sum)))

    side_rows = row_count // 2

    def row_part(rows):
        return (
            jnp.dot(gated[rows], fc2_share, preferred_element_type=jnp.float32)
            + jnp.dot(attended[rows], out_weight, preferred_element_type=jnp.float32)
        ).astype(jnp.bfloat16)

    far_out, near_out = row_part(slice(side_rows, None)), row_part(slice(0, side_rows))
    outputs = (tokens + reduce_rows(near_out, far_out) + out_bias + second_bias).astype(
        jnp.bfloat16
    )[None]

    def grad_part(rows):
        return (
            jnp.dot(grad_hidden[rows], fc1_share, preferred_element_type=jnp.float32)
            + lax.dot_general(
                grad_projected[rows],
                qkv_weight,
                contract_cols,
                preferred_element_type=jnp.float32,
            )
        ).astype(jnp.bfloat16)

    far_grad, near_grad = grad_part(slice(side_rows, None)), grad_part(slice(0, side_rows))
    grad_normed = reduce_rows(near_grad, far_grad)

    qkv_grad = lambda part: lax.dot_general(
        normed, part, contract_rows, preferred_element_type=jnp.float32
    ).astype(jnp.bfloat16)
    qkv_own, qkv_other = by_sides(own_pair, qkv_grad(back_mine), qkv_grad(back_returned))
    qkv_own = add_wide(qkv_own, swap_core(qkv_other)).astype(jnp.bfloat16)
    quarters = spread_over_cycle(qkv_own, 0)
    kind = lambda a, at: a[:, at * PAIR : (at + 1) * PAIR]
    qkv_rows = jnp.concatenate([kind(a, at) for at in range(3) for a in quarters], axis=1)
    own_width = model_width // devices
    by_wa = []
    for bits in range(4):
        piece = lax.dynamic_slice_in_dim(qkv_rows, (wa_at ^ bits) * own_width, own_width, 0)
        by_wa.append(swap(piece, "wa", bits) if bits else piece)
    y_near, y_far = by_sides(core, by_wa[0], by_wa[1]), by_sides(core, by_wa[2], by_wa[3])
    core_low, core_high = by_sides(y_at, y_near[0], y_far[0]), by_sides(y_at, y_near[1], y_far[1])
    sources = [core_low[0], core_high[0], core_low[1], core_high[1]]
    wide_kind = lambda a, at: a[:, at * 4 * PAIR : (at + 1) * 4 * PAIR]
    grad_qkv = jnp.concatenate(
        [wide_kind(a, at) for at in range(3) for a in sources], axis=1
    ).astype(jnp.float32)

    out_term = lax.dot_general(
        attended, grad_rows, contract_rows, preferred_element_type=jnp.float32
    )
    out_own_term = lax.dynamic_slice_in_dim(out_term, own_pair * PAIR, PAIR, 0)
    out_send = lax.dynamic_slice_in_dim(out_term, (1 - own_pair) * PAIR, PAIR, 0)
    out_own_term = add_wide(out_own_term, swap_core(out_send.astype(jnp.bfloat16)))
    head_keep = lax.dynamic_slice_in_dim(out_own_term, z_lo * HEAD_DIM, HEAD_DIM, 0)
    head_send = lax.dynamic_slice_in_dim(out_own_term, (1 - z_lo) * HEAD_DIM, HEAD_DIM, 0)
    head_sum = add_wide(head_keep, swap_zlo(head_send.astype(jnp.bfloat16)))
    routes = []
    for at in range(devices):
        bits = [(at >> shift) & 1 for shift in (4, 3, 2, 1, 0)]
        zh, zl, xx, yy, cc = bits
        routes.append((at, (((yy * 2 + cc) * 2 + zh) * 2 + xx) * 2 + zl))
    grad_out = lax.ppermute(head_sum.astype(jnp.bfloat16), both, routes).astype(jnp.float32)

    upstream_f32 = upstream.astype(jnp.float32)
    gain_term = jnp.sum(grad_normed * scaled, axis=0)
    shift_term = jnp.sum(grad_normed, axis=0)
    grad_scaled = grad_normed * gain_all
    grad_inputs = inverse * (
        grad_scaled
        - jnp.mean(grad_scaled, axis=1, keepdims=True)
        - scaled * jnp.mean(grad_scaled * scaled, axis=1, keepdims=True)
    )
    input_grads = (upstream_f32 + grad_inputs).astype(jnp.bfloat16)[None]

    pair_sums = jnp.sum(grad_projected.astype(jnp.float32), axis=0).reshape(2, 3, 1, PAIR)
    pair_sums = jnp.concatenate(by_sides(z_lo, pair_sums[0], pair_sums[1]), axis=1)
    in_y = (jnp.arange(2) == y_at).astype(jnp.float32)[None, :, None, None, None]
    in_quarter = (jnp.arange(4) == quarter).astype(jnp.float32)[None, None, None, :, None]
    qkv_sums = pair_sums[:, None, :, None, :] * in_y * in_quarter
    sums = jnp.concatenate(
        [
            gain_term.reshape(devices, -1),
            shift_term.reshape(devices, -1),
            jnp.sum(upstream_f32, axis=0).reshape(devices, -1),
            qkv_sums.reshape(devices, -1),
        ],
        axis=1,
    )
    sums = jnp.sum(lax.all_to_all(sums, both, 0, 0, tiled=True), axis=0)
    grad_ln_gain, grad_ln_bias, grad_b_out, grad_b_qkv = jnp.split(
        sums, [own_width, 2 * own_width, 3 * own_width]
    )
    return (
        outputs,
        input_grads,
        grad_ln_gain,
        grad_ln_bias,
        grad_qkv,
        grad_b_qkv,
        grad_out,
        grad_b_out,
        grad_fc1,
        grad_b_fc1,
        grad_fc2,
        grad_b_out,
    )


def solution(mesh):
    placed = (
        P("wa", "ctx", None),
        P("wa"),
        P("wa"),
        P("wa", None),
        P("wa"),
        P("wa", None),
        P("wa"),
        P("wa", None),
        P("wa"),
        P("wa", None),
        P("wa"),
        P("wa", "ctx", None),
    )

    def block(*arrays):
        rows = arrays[0].shape[1]
        on_cube = (mesh.shape["ctx"], mesh.shape["wa"], rows) == (8, 4, 2 * PIECE)
        if not on_cube:
            return on_device(*arrays)
        return on_cycle(*arrays)

    return jax.shard_map(
        block,
        mesh=mesh,
        in_specs=placed,
        out_specs=(
            P("wa", "ctx", None),
            P("wa", "ctx", None),
            P(("ctx", "wa")),
            P(("ctx", "wa")),
            P(("ctx", "wa"), None),
            P(("ctx", "wa")),
            P(("ctx", "wa"), None),
            P(("ctx", "wa")),
            P("wa", "ctx"),
            P("wa"),
            P("wa", "ctx"),
            P(("ctx", "wa")),
        ),
        check_vma=False,
    )
```
